32 devices in a mesh: shard: 16 (over z, y, x), head: 2 (over core).
Axes of the slice: x: 2, y: 2, z: 4, core: 2. Of those that a mesh axis runs over, the one named last changes fastest.
Arguments:
- queries: bfloat16 [8192, 2048], P('shard', 'head'), may hold values from -170 to 170
- key_weight: bfloat16 [1024, 2048], P('shard', 'head'), may hold values from -0.1875 to 0.1875
- value_weight: bfloat16 [1024, 2048], P('shard', 'head'), may hold values from -0.1875 to 0.1875
- out_weight: bfloat16 [4096, 2048], P(None, 'head'), may hold values from -0.5 to 0.5
- database: bfloat16 [64, 128, 1024], P('shard', 'head'), may hold values from -6 to 6
- neighbours: int32 [128, 2], replicated, may hold values from 0 to 63, as said below
- placement: int32 [64], replicated, may hold values from 0 to 63, as said below
Outputs:
- mixed: bfloat16 [8192, 4096], P('shard', 'head')
The draws below stay inside these ranges and needn't reach their ends.
Inputs may be any that keep to these rules, and one draw needn't show every extreme that they name: `placement`: each storage slot appears once; slot s is stored on index s // 4 of shard. The 16 neighbours of the groups of one index of shard have storage slots on pairwise different indices of shard.
All inputs are finite; a program needn't handle non-finite values.
Results may differ from the reference program's by a relative error of at most 0.012.
The reference program's roundings to bfloat16 on the way count: a program that leaves them out, or rounds other values in their place, can miss the bound.
Values may be sent and summed in bfloat16 or wider, within the bound.
A program may use at most 128 MiB of HBM per device.

```python
import jax
import jax.numpy as jnp
from jax import lax

D = 4096
HEADS = 16
HD = 128
DE = 1024
CH = 64
KNB = 2
R = 128
CH_DEV = 8
BLK_PER = 4
SEQ = 512
TOKENS = 8192
GROUPS = 128
NBLOCKS = 64
HDIM = 2048
N_SHARD = 16


def draw_queries(key, part):
    shape = (TOKENS, HEADS * HD)
    return jax.random.truncated_normal(key, -4.0, 4.0, shape, jnp.float32).astype(jnp.bfloat16)


def retrieval_tables(key):
    perm = jax.random.permutation(jax.random.fold_in(key, 11), NBLOCKS).astype(jnp.int32)
    source_weight = jax.random.randint(jax.random.fold_in(key, 12), (N_SHARD,), 1, 5).astype(jnp.int32)
    raw_score = jax.random.randint(jax.random.fold_in(key, 13), (N_SHARD, N_SHARD), 0, 1 << 20).astype(jnp.int32)
    score = raw_score * source_weight[None, :] * 128 + jnp.arange(N_SHARD, dtype=jnp.int32)[None, :]
    picks = KNB * CH_DEV
    unused, sources = lax.top_k(score, picks)
    sources = sources.astype(jnp.int32)
    within = jax.random.randint(jax.random.fold_in(key, 14), (N_SHARD, picks), 0, BLK_PER).astype(jnp.int32)
    slots = (sources * BLK_PER + within).reshape(GROUPS, KNB)
    inverse = jnp.zeros((NBLOCKS,), jnp.int32).at[perm].set(jnp.arange(NBLOCKS, dtype=jnp.int32))
    ids = inverse[slots].astype(jnp.int32)
    return (ids, perm)


def draw_neighbours(key, part):
    return retrieval_tables(key)[0]


def draw_placement(key, part):
    return retrieval_tables(key)[1]


def shard_levels(key, dims, shards, smallest, largest):
    def one(axis_at, blocks):
        steps = jax.random.uniform(jax.random.fold_in(jax.random.fold_in(key, 6), axis_at), (blocks,), jnp.float32, smallest / len(shards), largest / len(shards))
        return jnp.repeat(jnp.exp(steps), dims[axis_at] // blocks).reshape((-1,) + (1,) * (len(dims) - axis_at - 1))

    level = one(*shards[0])
    for cut in shards[1:]:
        level = level * one(*cut)
    return level


def gaussian(own_key, dims, spread, limit, shards=(), kind=jnp.bfloat16):
    array = spread * jax.random.normal(own_key, dims, jnp.float32)
    if shards:
        array = array * shard_levels(own_key, dims, shards, -0.22, 0.18)
    return jnp.clip(array, -limit, limit).astype(kind)


def setup_inputs(seed: int = 0) -> dict:
    seeds = jax.random.split(jax.random.key(seed), 8)
    queries = draw_queries(jax.random.fold_in(seeds[7], 71), 0)
    key_weight = gaussian(seeds[1], (DE, HDIM), DE ** -0.5, 0.1875, ((0, 16), (1, 2)))
    value_weight = gaussian(seeds[2], (DE, HDIM), DE ** -0.5, 0.1875, ((0, 16), (1, 2)))
    out_weight = gaussian(seeds[3], (D, HDIM), HD ** -0.5, 0.5, ((1, 2),))
    database = gaussian(seeds[4], (NBLOCKS, R, DE), 1.0, 6.0, ((0, 16), (1, 2)))
    neighbours = draw_neighbours(jax.random.fold_in(seeds[7], 71), 0)
    placement = draw_placement(jax.random.fold_in(seeds[7], 71), 0)
    return {"queries": queries, "key_weight": key_weight, "value_weight": value_weight, "out_weight": out_weight, "database": database, "neighbours": neighbours, "placement": placement}


def reference(queries, key_weight, value_weight, out_weight, database, neighbours, placement):
    head_width = HEADS * HD
    seq_count = TOKENS // SEQ
    score_scale = HD ** -0.5
    block_rows = placement[neighbours].astype(jnp.int32)
    query_seq = queries.reshape(seq_count, SEQ, head_width)
    query_pad = jnp.concatenate([query_seq[:, CH - 1:], jnp.zeros((seq_count, CH - 1, head_width), jnp.bfloat16)], axis=1)
    query_pad = query_pad.reshape(GROUPS, CH, HEADS, HD)

    def one_group(pair_args):
        query_win, slot_pair = pair_args
        encoded = database[slot_pair].reshape(KNB * R, DE)
        key_rows = jnp.dot(encoded, key_weight, preferred_element_type=jnp.float32).astype(jnp.bfloat16)
        val_rows = jnp.dot(encoded, value_weight, preferred_element_type=jnp.float32).astype(jnp.bfloat16)
        key_rows = key_rows.reshape(KNB * R, HEADS, HD)
        val_rows = val_rows.reshape(KNB * R, HEADS, HD)
        scores = jnp.einsum("whd,khd->hwk", query_win.astype(jnp.float32), key_rows.astype(jnp.float32)) * score_scale
        row_max = jnp.max(scores, axis=-1, keepdims=True)
        expo = jnp.exp(scores - row_max)
        probs = expo / jnp.sum(expo, axis=-1, keepdims=True)
        weights_bf = probs.astype(jnp.bfloat16)
        window_out = jnp.einsum("hwk,khd->whd", weights_bf.astype(jnp.float32), val_rows.astype(jnp.float32))
        return window_out.astype(jnp.bfloat16).reshape(CH, head_width)

    windows = lax.map(one_group, (query_pad, block_rows))
    windows = windows.reshape(seq_count, SEQ, head_width)
    attention = jnp.concatenate([jnp.zeros((seq_count, CH - 1, head_width), jnp.bfloat16), windows[:, :SEQ - (CH - 1)]], axis=1)
    attention = attention.reshape(TOKENS, head_width)
    mixed_out = lax.dot_general(attention, out_weight, (((1,), (1,)), ((), ())), preferred_element_type=jnp.float32)
    return mixed_out.astype(jnp.bfloat16)
```

```python
import jax
import jax.numpy as jnp
from jax import lax
from jax.experimental import pallas as pl
from jax.experimental.pallas import tpu as pltpu
from jax.sharding import PartitionSpec as P

HD = 128
CH = 64
KNB = 2
NZ, NY, NX = 4, 2, 2
MESH = pl.DeviceIdType.MESH
VMEM_LIMIT = 60 * 1024 * 1024
NT = (((1,), (1,)), ((), ()))


def shifted(shard, dz, dy, dx):
    z, y, x = shard // (NY * NX), (shard // NX) % NY, shard % NX
    return ((z + dz) % NZ) * (NY * NX) + ((y + dy) % NY) * NX + (x + dx) % NX


def fused_kernel(
    which_ref, slot_ref, q_ref, kw_ref, vw_ref, ow_ref, db_ref,
    att_ref, ow_recv,
    w, e_out, e_in, kk, vv,
    a_send, a_recv, f_send, f_recv, z_send, p_send, g_send, w_recv, o_sem, t_send, t_recv,
):
    s = lax.axis_index("shard")
    h = lax.axis_index("head")
    z, y, x = s // (NY * NX), (s // NX) % NY, s % NX
    near_x = s + 1 - 2 * x
    near_y = s + NX * (1 - 2 * y)
    plane = NY * NX
    n = NZ * NY * NX
    half, de = db_ref.shape[1], db_ref.shape[2]
    width = q_ref.shape[1]
    feats = ow_recv.shape[0]

    barrier = pltpu.get_barrier_semaphore()
    for d in range(1, n):
        to = shifted(s, d // plane, (d // NX) % NY, d % NX)
        pl.semaphore_signal(barrier, inc=1, device_id=(to, h), device_id_type=MESH)
    pl.semaphore_signal(barrier, inc=1, device_id=(s, 1 - h), device_id_type=MESH)
    w[0, s] = kw_ref[...]
    w[1, s] = vw_ref[...]
    for d in range(1, n):
        e_out[d] = db_ref[which_ref[d]]
    e_in[0, h] = db_ref[which_ref[0]]
    pl.semaphore_wait(barrier, n)

    def weight_copy(kind, chunk, to, sem):
        return pltpu.make_async_remote_copy(
            src_ref=w.at[kind, chunk], dst_ref=w.at[kind, chunk], send_sem=sem,
            recv_sem=w_recv.at[kind, chunk], device_id=(to, h), device_id_type=MESH)

    def up_copy(kind, zz):
        return weight_copy(kind, zz * plane + y * NX + x, s + plane, z_send.at[0, kind, zz])

    def down_copy(kind, zz):
        return weight_copy(kind, zz * plane + y * NX + x, s - plane, z_send.at[1, kind, zz])

    def x_copy(kind, zz):
        return weight_copy(kind, zz * plane + y * NX + x, near_x, p_send.at[0, kind, zz])

    def y_copy(kind, zz):
        return weight_copy(kind, zz * plane + y * NX + x, near_y, p_send.at[1, kind, zz])

    def diag_k(zz):
        return weight_copy(0, zz * plane + y * NX + 1 - x, near_y, g_send.at[0, zz])

    def diag_v(zz):
        return weight_copy(1, zz * plane + (1 - y) * NX + x, near_x, g_send.at[1, zz])

    def arrive(kind, chunk):
        weight_copy(kind, chunk, near_x, z_send.at[0, 0, 0]).wait_recv()

    def enc_copy(d):
        to = shifted(s, d // plane, (d // NX) % NY, d % NX)
        return pltpu.make_async_remote_copy(
            src_ref=e_out.at[d], dst_ref=e_in.at[d, h], send_sem=a_send.at[d],
            recv_sem=a_recv.at[d], device_id=(to, h), device_id_type=MESH)

    def half_copy(d):
        return pltpu.make_async_remote_copy(
            src_ref=e_in.at[d, h], dst_ref=e_in.at[d, h], send_sem=f_send.at[d],
            recv_sem=f_recv.at[d], device_id=(s, 1 - h), device_id_type=MESH)

    def half_arrive(d):
        pltpu.make_async_remote_copy(
            src_ref=e_in.at[d, 1 - h], dst_ref=e_in.at[d, 1 - h], send_sem=f_send.at[d],
            recv_sem=f_recv.at[d], device_id=(s, 1 - h), device_id_type=MESH).wait_recv()

    def out_copy():
        return pltpu.make_async_remote_copy(
            src_ref=ow_ref.at[pl.ds((1 - h) * feats, feats), :], dst_ref=ow_recv,
            send_sem=o_sem.at[0], recv_sem=o_sem.at[1], device_id=(s, 1 - h),
            device_id_type=MESH)

    for kind in range(2):
        @pl.when(z < NZ - 1)
        def _():
            up_copy(kind, z).start()

        @pl.when(z > 0)
        def _():
            down_copy(kind, z).start()
        x_copy(kind, z).start()
        y_copy(kind, z).start()
    for dz in (2, 1, 3, 0):
        for d in range(dz * plane, (dz + 1) * plane):
            if d:
                enc_copy(d).start()
    half_copy(0).start()
    out_copy().start()

    def turn(zz):
        arrive(0, zz * plane + y * NX + 1 - x)
        diag_k(zz).start()
        arrive(1, zz * plane + (1 - y) * NX + x)
        diag_v(zz).start()

    def pass_halves(dz):
        for d in range(dz * plane, (dz + 1) * plane):
            if d:
                enc_copy(d).wait_recv()
                half_copy(d).start()

    for k in range(1, NZ + 1):
        if k < NZ:
            @pl.when(z >= k)
            def _():
                for kind in range(2):
                    arrive(kind, (z - k) * plane + y * NX + x)

                    @pl.when(z < NZ - 1)
                    def _():
                        up_copy(kind, z - k).start()
                    x_copy(kind, z - k).start()
                    y_copy(kind, z - k).start()

            @pl.when(z + k < NZ)
            def _():
                for kind in range(2):
                    arrive(kind, (z + k) * plane + y * NX + x)

                    @pl.when(z > 0)
                    def _():
                        down_copy(kind, z + k).start()
                    x_copy(kind, z + k).start()
                    y_copy(kind, z + k).start()
        if k == 1:
            turn(z)
        else:
            @pl.when(z >= k - 1)
            def _():
                turn(z - (k - 1))

            @pl.when(z + k - 1 < NZ)
            def _():
                turn(z + k - 1)
    for zz in range(NZ):
        arrive(1, zz * plane + y * NX + 1 - x)
        arrive(0, zz * plane + (1 - y) * NX + x)
        for kind in range(2):
            arrive(kind, zz * plane + (1 - y) * NX + 1 - x)

    order = (0, 1, 3, 2)
    tile = 256
    pass_halves(order[0])
    for i, dz in enumerate(order):
        if i + 1 < NZ:
            pass_halves(order[i + 1])
        for d in range(dz * plane, (dz + 1) * plane):
            half_arrive(d)

        @pl.loop(0, width // tile)
        def _(c):
            cols = pl.ds(pl.multiple_of(c * tile, tile), tile)
            enc = e_in[dz * plane:(dz + 1) * plane].reshape(plane * 2 * half, de)
            for kind, dst in ((0, kk), (1, vv)):
                rows = w[kind, :, :, cols].reshape(de, tile)
                got = jnp.dot(enc, rows, preferred_element_type=jnp.float32)
                dst[dz * plane:(dz + 1) * plane, :, cols] = got.astype(jnp.bfloat16).reshape(
                    plane, 2 * half, tile)

    scale = HD ** -0.5
    groups = q_ref.shape[0] // CH
    edge = 16

    def attend(c, start, count):
        one = slot_ref[KNB * c]
        two = slot_ref[KNB * c + 1]
        for head in range(width // HD):
            cols = slice(head * HD, (head + 1) * HD)
            q = q_ref[pl.ds(start, count), cols]
            score = jnp.concatenate(
                [lax.dot_general(q, kk[one, :, cols], NT, preferred_element_type=jnp.float32),
                 lax.dot_general(q, kk[two, :, cols], NT, preferred_element_type=jnp.float32)],
                axis=1) * scale
            expo = jnp.exp(score - jnp.max(score, axis=1, keepdims=True))
            weight = (expo / jnp.sum(expo, axis=1, keepdims=True)).astype(jnp.bfloat16)
            value = jnp.concatenate([vv[one, :, cols], vv[two, :, cols]], axis=0)
            got = jnp.dot(weight, value, preferred_element_type=jnp.float32)
            last = lax.broadcasted_iota(jnp.int32, (edge, HD), 0) == edge - 1
            old = att_ref[0, pl.ds(start, edge), cols].astype(jnp.float32)
            att_ref[0, pl.ds(start, edge), cols] = jnp.where(last, got[:edge], old).astype(jnp.bfloat16)
            if count > edge:
                att_ref[0, pl.ds(pl.multiple_of(start + edge, edge), count - edge), cols] = (
                    got[edge:].astype(jnp.bfloat16))

    def swap(c):
        rows = pl.ds(pl.multiple_of(c * CH, CH), CH)
        return pltpu.make_async_remote_copy(
            src_ref=att_ref.at[0, rows], dst_ref=att_ref.at[1, rows], send_sem=t_send.at[c],
            recv_sem=t_recv.at[c], device_id=(s, 1 - h), device_id_type=MESH)

    att_ref[0, 0:CH] = jnp.zeros((CH, width), jnp.bfloat16)

    @pl.loop(0, groups - 1)
    def _(c):
        attend(c, pl.multiple_of(c * CH + CH - edge, edge), CH + edge)
        swap(c).start()

    attend(groups - 1, groups * CH - edge, edge)
    swap(groups - 1).start()

    for zz in range(NZ):
        for kind in range(2):
            @pl.when(z < NZ - 1)
            def _():
                @pl.when(z >= zz)
                def _():
                    up_copy(kind, zz).wait_send()

            @pl.when(z > 0)
            def _():
                @pl.when(z <= zz)
                def _():
                    down_copy(kind, zz).wait_send()
            x_copy(kind, zz).wait_send()
            y_copy(kind, zz).wait_send()
        diag_k(zz).wait_send()
        diag_v(zz).wait_send()
    for d in range(n):
        if d:
            enc_copy(d).wait_send()
        half_copy(d).wait_send()
    out_copy().wait()
    for c in range(groups):
        swap(c).wait()


def project_kernel(side_ref, att_ref, own_ref, other_ref, out_ref):
    out_ref[...] = (
        lax.dot_general(att_ref[0], own_ref[...], NT, preferred_element_type=jnp.float32)
        + lax.dot_general(att_ref[1], other_ref[...], NT, preferred_element_type=jnp.float32)
    ).astype(jnp.bfloat16)


def local_small(queries, key_weight, value_weight, out_weight, database, neighbours, placement):
    n = NZ * NY * NX
    s = lax.axis_index("shard")
    h = lax.axis_index("head")
    tok, width = queries.shape
    blk, half, de = database.shape
    feats = out_weight.shape[0] // 2
    nblocks = placement.shape[0]
    ids = jnp.arange(nblocks, dtype=jnp.int32)
    needed = neighbours.reshape(n, -1)
    slots = jnp.sum(jnp.where(needed[:, :, None] == ids, placement, 0), axis=-1)
    owners = slots // blk
    offs = jnp.arange(n, dtype=jnp.int32)
    dests = shifted(s, offs // (NY * NX), (offs // NX) % NY, offs % NX)
    pick = (dests[:, None, None] == offs[None, :, None]) & (owners == s)[None]
    which = jnp.sum(jnp.where(pick, (slots % blk)[None], 0), axis=(1, 2))
    own = jnp.sum(jnp.where((offs == s)[:, None], owners, 0), axis=0)
    slot = (
        ((s // 4 - own // 4) % NZ) * 4 + ((s // 2 - own // 2) % NY) * 2 + (s - own) % NX
    ).astype(jnp.int32)
    vm = pl.BlockSpec(memory_space=pltpu.VMEM)
    sm = pl.BlockSpec(memory_space=pltpu.SMEM)
    hbm = pl.BlockSpec(memory_space=pl.ANY)
    dma = pltpu.SemaphoreType.DMA
    att, ow_recv = pl.pallas_call(
        fused_kernel,
        out_shape=(
            jax.ShapeDtypeStruct((2, tok, width), jnp.bfloat16),
            jax.ShapeDtypeStruct((feats, width), jnp.bfloat16),
        ),
        in_specs=[sm, sm, vm, vm, vm, hbm, vm],
        out_specs=(vm, hbm),
        scratch_shapes=[
            pltpu.VMEM((2, n) + key_weight.shape, jnp.bfloat16),
            pltpu.VMEM((n, half, de), jnp.bfloat16),
            pltpu.VMEM((n, 2, half, de), jnp.bfloat16),
            pltpu.VMEM((n, 2 * half, width), jnp.bfloat16),
            pltpu.VMEM((n, 2 * half, width), jnp.bfloat16),
            dma((n,)), dma((n,)), dma((n,)), dma((n,)),
            dma((2, 2, NZ)), dma((2, 2, NZ)), dma((2, NZ)), dma((2, n)),
            dma((2,)), dma((tok // CH,)), dma((tok // CH,)),
        ],
        compiler_params=pltpu.CompilerParams(
            collective_id=0, has_side_effects=True, vmem_limit_bytes=VMEM_LIMIT),
    )(which.astype(jnp.int32), slot, queries, key_weight, value_weight, out_weight, database)
    tile = 256
    steps = feats // tile
    return pl.pallas_call(
        project_kernel,
        out_shape=jax.ShapeDtypeStruct((tok, feats), jnp.bfloat16),
        grid_spec=pltpu.PrefetchScalarGridSpec(
            num_scalar_prefetch=1,
            grid=(steps,),
            in_specs=[
                pl.BlockSpec((2, tok, width), lambda i, side: (0, 0, 0)),
                pl.BlockSpec((tile, width), lambda i, side: (side[0] * steps + i, 0)),
                pl.BlockSpec((tile, width), lambda i, side: (i, 0)),
            ],
            out_specs=pl.BlockSpec((tok, tile), lambda i, side: (0, i)),
        ),
        compiler_params=pltpu.CompilerParams(vmem_limit_bytes=VMEM_LIMIT),
    )(h.astype(jnp.int32).reshape(1), att, out_weight, ow_recv)


def local_general(queries, key_weight, value_weight, out_weight, database, neighbours, placement):
    shard_count = lax.axis_size("shard")
    shard_self = lax.axis_index("shard")
    tok_rows = queries.shape[0]
    hd_local = queries.shape[1]
    heads_local = hd_local // HD
    per_dev = tok_rows // CH
    blk_local = database.shape[0]
    slots = placement[neighbours]
    needed = slots.reshape(shard_count, per_dev * KNB)
    owners = needed // blk_local
    matches = owners == shard_self
    hits = jnp.any(matches, axis=1)
    which = jnp.sum(jnp.where(matches, needed % blk_local, 0), axis=1)
    outgoing = jnp.where(hits[:, None, None], database[which], jnp.zeros((), jnp.bfloat16))
    arrived = lax.all_to_all(outgoing, "shard", split_axis=0, concat_axis=0, tiled=True)
    own_need = lax.dynamic_slice_in_dim(needed, shard_self, 1, 0)[0]
    half_rows = arrived[own_need // blk_local]
    encoded = lax.all_gather(half_rows, "head", axis=1, tiled=True)
    key_rows, val_rows = (
        lax.all_gather(key_weight, "shard", axis=0, tiled=True),
        lax.all_gather(value_weight, "shard", axis=0, tiled=True),
    )
    key_block = jnp.einsum(
        "brd,de->bre", encoded, key_rows, preferred_element_type=jnp.float32
    ).astype(jnp.bfloat16)
    val_block = jnp.einsum(
        "brd,de->bre", encoded, val_rows, preferred_element_type=jnp.float32
    ).astype(jnp.bfloat16)
    neighbour_len = encoded.shape[1]
    key_heads = key_block.reshape(per_dev, KNB * neighbour_len, heads_local, HD)
    val_heads = val_block.reshape(per_dev, KNB * neighbour_len, heads_local, HD)
    query_pad = jnp.concatenate(
        [queries[CH - 1 :], jnp.zeros((CH - 1, hd_local), jnp.bfloat16)], axis=0
    )
    query_pad = query_pad.reshape(per_dev, CH, heads_local, HD)
    score_scale = HD ** (-0.5)
    scores = (
        jnp.einsum("swhd,skhd->shwk", query_pad, key_heads, preferred_element_type=jnp.float32)
        * score_scale
    )
    row_max = jnp.max(scores, axis=-1, keepdims=True)
    expo = jnp.exp(scores - row_max)
    probs = expo / jnp.sum(expo, axis=-1, keepdims=True)
    weights_bf = probs.astype(jnp.bfloat16)
    window_out = jnp.einsum(
        "shwk,skhd->swhd", weights_bf, val_heads, preferred_element_type=jnp.float32
    )
    window_rows = window_out.astype(jnp.bfloat16).reshape(tok_rows, hd_local)
    attention = jnp.concatenate(
        [jnp.zeros((CH - 1, hd_local), jnp.bfloat16), window_rows[: tok_rows - (CH - 1)]], axis=0
    )
    partial_value = lax.dot_general(
        attention, out_weight, (((1,), (1,)), ((), ())), preferred_element_type=jnp.float32
    )
    return lax.psum_scatter(partial_value, "head", scatter_dimension=1, tiled=True).astype(
        jnp.bfloat16
    )


def solution(mesh):
    sizes = dict(mesh.shape)
    small = sizes["shard"] == NZ * NY * NX and sizes["head"] == 2
    return jax.shard_map(
        local_small if small else local_general,
        mesh=mesh,
        in_specs=(
            P("shard", "head"),
            P("shard", "head"),
            P("shard", "head"),
            P(None, "head"),
            P("shard", "head", None),
            P(),
            P(),
        ),
        out_specs=P("shard", "head"),
        check_vma=False,
    )
```

```python
import jax
import jax.numpy as jnp
from jax import lax
from jax.experimental import pallas as pl
from jax.experimental.pallas import tpu as pltpu
from jax.sharding import PartitionSpec as P

HD = 128
CH = 64
KNB = 2
NZ, NY, NX = 4, 2, 2
MESH = pl.DeviceIdType.MESH
VMEM_LIMIT = 60 * 1024 * 1024
NT = (((1,), (1,)), ((), ()))


def shifted(shard, dz, dy, dx):
    z, y, x = shard // (NY * NX), (shard // NX) % NY, shard % NX
    return ((z + dz) % NZ) * (NY * NX) + ((y + dy) % NY) * NX + (x + dx) % NX


def fused_kernel(
    which_ref, slot_ref, q_ref, kw_ref, vw_ref, ow_ref, db_ref,
    att_ref, ow_recv,
    w, up_1, up_2, up_3, down_1, down_2, down_3, e_out, e_in, kk, vv,
    d_send, d_recv, a_send, a_recv, f_send, f_recv, z_send, p_send, g_send, w_recv, o_sem,
    t_send, t_recv,
):
    s = lax.axis_index("shard")
    h = lax.axis_index("head")
    z, y, x = s // (NY * NX), (s // NX) % NY, s % NX
    near_x = s + 1 - 2 * x
    near_y = s + NX * (1 - 2 * y)
    plane = NY * NX
    n = NZ * NY * NX
    half, de = db_ref.shape[1], db_ref.shape[2]
    width = q_ref.shape[1]
    feats = ow_recv.shape[0]

    barrier = pltpu.get_barrier_semaphore()
    for d in range(1, n):
        to = shifted(s, d // plane, (d // NX) % NY, d % NX)
        pl.semaphore_signal(barrier, inc=1, device_id=(to, h), device_id_type=MESH)
    pl.semaphore_signal(barrier, inc=1, device_id=(s, 1 - h), device_id_type=MESH)
    w[0, s] = kw_ref[...]
    w[1, s] = vw_ref[...]
    pl.semaphore_wait(barrier, n)
    ups = (db_ref, up_1, up_2, up_3)
    downs = (db_ref, down_1, down_2, down_3)

    def weight_copy(kind, chunk, to, sem):
        return pltpu.make_async_remote_copy(
            src_ref=w.at[kind, chunk], dst_ref=w.at[kind, chunk], send_sem=sem,
            recv_sem=w_recv.at[kind, chunk], device_id=(to, h), device_id_type=MESH)

    def up_copy(kind, zz):
        return weight_copy(kind, zz * plane + y * NX + x, s + plane, z_send.at[0, kind, zz])

    def down_copy(kind, zz):
        return weight_copy(kind, zz * plane + y * NX + x, s - plane, z_send.at[1, kind, zz])

    def x_copy(kind, zz):
        return weight_copy(kind, zz * plane + y * NX + x, near_x, p_send.at[0, kind, zz])

    def y_copy(kind, zz):
        return weight_copy(kind, zz * plane + y * NX + x, near_y, p_send.at[1, kind, zz])

    def diag_k(zz):
        return weight_copy(0, zz * plane + y * NX + 1 - x, near_y, g_send.at[0, zz])

    def diag_v(zz):
        return weight_copy(1, zz * plane + (1 - y) * NX + x, near_x, g_send.at[1, zz])

    def arrive(kind, chunk):
        weight_copy(kind, chunk, near_x, z_send.at[0, 0, 0]).wait_recv()

    def set_up(k):
        return pltpu.make_async_remote_copy(
            src_ref=ups[k], dst_ref=ups[k + 1], send_sem=d_send.at[0, k],
            recv_sem=d_recv.at[0, k + 1], device_id=(s + plane, h), device_id_type=MESH)

    def set_down(k):
        return pltpu.make_async_remote_copy(
            src_ref=downs[k], dst_ref=downs[k + 1], send_sem=d_send.at[1, k],
            recv_sem=d_recv.at[1, k + 1], device_id=(s - plane, h), device_id_type=MESH)

    def enc_copy(zz, j):
        to = shifted(s, 0, j // NX, j % NX)
        d = zz * plane + j
        return pltpu.make_async_remote_copy(
            src_ref=e_out.at[d], dst_ref=e_in.at[d, h], send_sem=a_send.at[d],
            recv_sem=a_recv.at[d], device_id=(to, h), device_id_type=MESH)

    def spread(zz, held):
        for j in range(1, plane):
            d = zz * plane + j
            e_out[d] = held[which_ref[d]]
            enc_copy(zz, j).start()
        e_in[zz * plane, h] = held[which_ref[zz * plane]]
        half_copy(zz * plane).start()

    def sets(k):
        @pl.when(z >= k)
        def _():
            set_up(k - 1).wait_recv()
            if k < NZ - 1:
                @pl.when(z < NZ - 1)
                def _():
                    set_up(k).start()
            spread(z - k, ups[k])

        @pl.when(z + k < NZ)
        def _():
            set_down(k - 1).wait_recv()
            if k < NZ - 1:
                @pl.when(z > 0)
                def _():
                    set_down(k).start()
            spread(z + k, downs[k])

    def half_copy(d):
        return pltpu.make_async_remote_copy(
            src_ref=e_in.at[d, h], dst_ref=e_in.at[d, h], send_sem=f_send.at[d],
            recv_sem=f_recv.at[d], device_id=(s, 1 - h), device_id_type=MESH)

    def half_arrive(d):
        pltpu.make_async_remote_copy(
            src_ref=e_in.at[d, 1 - h], dst_ref=e_in.at[d, 1 - h], send_sem=f_send.at[d],
            recv_sem=f_recv.at[d], device_id=(s, 1 - h), device_id_type=MESH).wait_recv()

    def out_copy():
        return pltpu.make_async_remote_copy(
            src_ref=ow_ref.at[pl.ds((1 - h) * feats, feats), :], dst_ref=ow_recv,
            send_sem=o_sem.at[0], recv_sem=o_sem.at[1], device_id=(s, 1 - h),
            device_id_type=MESH)

    for kind in range(2):
        @pl.when(z < NZ - 1)
        def _():
            up_copy(kind, z).start()

        @pl.when(z > 0)
        def _():
            down_copy(kind, z).start()
        x_copy(kind, z).start()
        y_copy(kind, z).start()
    spread(z, db_ref)
    out_copy().start()

    def turn(zz):
        arrive(0, zz * plane + y * NX + 1 - x)
        diag_k(zz).start()
        arrive(1, zz * plane + (1 - y) * NX + x)
        diag_v(zz).start()

    def pass_halves(zz):
        for j in range(1, plane):
            enc_copy(zz, j).wait_recv()
            half_copy(zz * plane + j).start()

    for k in range(1, NZ + 1):
        if k < NZ:
            @pl.when(z >= k)
            def _():
                for kind in range(2):
                    arrive(kind, (z - k) * plane + y * NX + x)

                    @pl.when(z < NZ - 1)
                    def _():
                        up_copy(kind, z - k).start()
                    x_copy(kind, z - k).start()
                    y_copy(kind, z - k).start()

            @pl.when(z + k < NZ)
            def _():
                for kind in range(2):
                    arrive(kind, (z + k) * plane + y * NX + x)

                    @pl.when(z > 0)
                    def _():
                        down_copy(kind, z + k).start()
                    x_copy(kind, z + k).start()
                    y_copy(kind, z + k).start()
        if k == 1:
            @pl.when(z < NZ - 1)
            def _():
                set_up(0).start()

            @pl.when(z > 0)
            def _():
                set_down(0).start()
            turn(z)
        else:
            @pl.when(z >= k - 1)
            def _():
                turn(z - (k - 1))

            @pl.when(z + k - 1 < NZ)
            def _():
                turn(z + k - 1)
        if 2 <= k < NZ:
            sets(k - 1)
    for zz in range(NZ):
        arrive(1, zz * plane + y * NX + 1 - x)
        arrive(0, zz * plane + (1 - y) * NX + x)
        for kind in range(2):
            arrive(kind, zz * plane + (1 - y) * NX + 1 - x)

    tile = 256

    def project(zz):
        for j in range(plane):
            half_arrive(zz * plane + j)
        slab = pl.ds(zz * plane, plane)

        @pl.loop(0, width // tile)
        def _(c):
            cols = pl.ds(pl.multiple_of(c * tile, tile), tile)
            enc = e_in[slab].reshape(plane * 2 * half, de)
            for kind, dst in ((0, kk), (1, vv)):
                rows = w[kind, :, :, cols].reshape(de, tile)
                got = jnp.dot(enc, rows, preferred_element_type=jnp.float32)
                dst[slab, :, cols] = got.astype(jnp.bfloat16).reshape(plane, 2 * half, tile)

    def each(k, act):
        @pl.when(z >= k)
        def _():
            act(z - k)

        @pl.when(z + k < NZ)
        def _():
            act(z + k)

    pass_halves(z)
    project(z)
    for k in range(1, NZ):
        each(k, pass_halves)
        if k == NZ - 2:
            sets(NZ - 1)
        each(k, project)

    scale = HD ** -0.5
    groups = q_ref.shape[0] // CH
    edge = 16

    def attend(c, start, count):
        one = slot_ref[KNB * c]
        two = slot_ref[KNB * c + 1]
        last = lax.broadcasted_iota(jnp.int32, (edge, HD), 0) == edge - 1
        batch = 4
        for first in range(0, width // HD, batch):
            spans = [slice(i * HD, (i + 1) * HD) for i in range(first, first + batch)]
            scores = []
            for cols in spans:
                q = q_ref[pl.ds(start, count), cols]
                keys = jnp.concatenate([kk[one, :, cols], kk[two, :, cols]], axis=0)
                scores.append(
                    lax.dot_general(q, keys, NT, preferred_element_type=jnp.float32) * scale)
            tops = [jnp.max(score, axis=1, keepdims=True) for score in scores]
            expos = [jnp.exp(score - top) for score, top in zip(scores, tops)]
            sums = [jnp.sum(expo, axis=1, keepdims=True) for expo in expos]
            weights = [(expo / total).astype(jnp.bfloat16) for expo, total in zip(expos, sums)]
            outs = []
            for cols, weight in zip(spans, weights):
                value = jnp.concatenate([vv[one, :, cols], vv[two, :, cols]], axis=0)
                outs.append(jnp.dot(weight, value, preferred_element_type=jnp.float32))
            for cols, got in zip(spans, outs):
                old = att_ref[0, pl.ds(start, edge), cols].astype(jnp.float32)
                att_ref[0, pl.ds(start, edge), cols] = jnp.where(last, got[:edge], old).astype(
                    jnp.bfloat16)
                if count > edge:
                    att_ref[0, pl.ds(pl.multiple_of(start + edge, edge), count - edge), cols] = (
                        got[edge:].astype(jnp.bfloat16))

    def swap(c):
        rows = pl.ds(pl.multiple_of(c * CH, CH), CH)
        return pltpu.make_async_remote_copy(
            src_ref=att_ref.at[0, rows], dst_ref=att_ref.at[1, rows], send_sem=t_send.at[c],
            recv_sem=t_recv.at[c], device_id=(s, 1 - h), device_id_type=MESH)

    att_ref[0, 0:CH] = jnp.zeros((CH, width), jnp.bfloat16)

    @pl.loop(0, groups - 1)
    def _(c):
        attend(c, pl.multiple_of(c * CH + CH - edge, edge), CH + edge)
        swap(c).start()

    attend(groups - 1, groups * CH - edge, edge)
    swap(groups - 1).start()

    for zz in range(NZ):
        for kind in range(2):
            @pl.when(z < NZ - 1)
            def _():
                @pl.when(z >= zz)
                def _():
                    up_copy(kind, zz).wait_send()

            @pl.when(z > 0)
            def _():
                @pl.when(z <= zz)
                def _():
                    down_copy(kind, zz).wait_send()
            x_copy(kind, zz).wait_send()
            y_copy(kind, zz).wait_send()
        diag_k(zz).wait_send()
        diag_v(zz).wait_send()
    for k in range(NZ - 1):
        @pl.when(z < NZ - 1)
        def _():
            @pl.when(z >= k)
            def _():
                set_up(k).wait_send()

        @pl.when(z > 0)
        def _():
            @pl.when(z + k < NZ)
            def _():
                set_down(k).wait_send()
    for zz in range(NZ):
        for j in range(plane):
            if j:
                enc_copy(zz, j).wait_send()
            half_copy(zz * plane + j).wait_send()
    out_copy().wait()
    for c in range(groups):
        swap(c).wait()


def project_kernel(side_ref, att_ref, own_ref, other_ref, out_ref):
    out_ref[...] = (
        lax.dot_general(att_ref[0], own_ref[...], NT, preferred_element_type=jnp.float32)
        + lax.dot_general(att_ref[1], other_ref[...], NT, preferred_element_type=jnp.float32)
    ).astype(jnp.bfloat16)


def local_small(queries, key_weight, value_weight, out_weight, database, neighbours, placement):
    n = NZ * NY * NX
    s = lax.axis_index("shard")
    h = lax.axis_index("head")
    tok, width = queries.shape
    blk, half, de = database.shape
    feats = out_weight.shape[0] // 2
    nblocks = placement.shape[0]
    ids = jnp.arange(nblocks, dtype=jnp.int32)
    needed = neighbours.reshape(n, -1)
    slots = jnp.sum(jnp.where(needed[:, :, None] == ids, placement, 0), axis=-1)
    owners = slots // blk
    offs = jnp.arange(n, dtype=jnp.int32)
    plane = NY * NX
    dests = shifted(s, 0, (offs // NX) % NY, offs % NX)
    origin = offs // plane * plane + s % plane
    pick = (dests[:, None, None] == offs[None, :, None]) & (owners[None] == origin[:, None, None])
    which = jnp.sum(jnp.where(pick, (slots % blk)[None], 0), axis=(1, 2))
    own = jnp.sum(jnp.where((offs == s)[:, None], owners, 0), axis=0)
    slot = (
        own // plane * plane + (s // NX + own // NX) % NY * NX + (s + own) % NX
    ).astype(jnp.int32)
    vm = pl.BlockSpec(memory_space=pltpu.VMEM)
    sm = pl.BlockSpec(memory_space=pltpu.SMEM)
    hbm = pl.BlockSpec(memory_space=pl.ANY)
    dma = pltpu.SemaphoreType.DMA
    att, ow_recv = pl.pallas_call(
        fused_kernel,
        out_shape=(
            jax.ShapeDtypeStruct((2, tok, width), jnp.bfloat16),
            jax.ShapeDtypeStruct((feats, width), jnp.bfloat16),
        ),
        in_specs=[sm, sm, vm, vm, vm, hbm, vm],
        out_specs=(vm, hbm),
        scratch_shapes=[
            pltpu.VMEM((2, n) + key_weight.shape, jnp.bfloat16),
            *[pltpu.VMEM(database.shape, jnp.bfloat16)] * 6,
            pltpu.VMEM((n, half, de), jnp.bfloat16),
            pltpu.VMEM((n, 2, half, de), jnp.bfloat16),
            pltpu.VMEM((n, 2 * half, width), jnp.bfloat16),
            pltpu.VMEM((n, 2 * half, width), jnp.bfloat16),
            dma((2, NZ)), dma((2, NZ)), dma((n,)), dma((n,)), dma((n,)), dma((n,)),
            dma((2, 2, NZ)), dma((2, 2, NZ)), dma((2, NZ)), dma((2, n)),
            dma((2,)), dma((tok // CH,)), dma((tok // CH,)),
        ],
        compiler_params=pltpu.CompilerParams(
            collective_id=0, has_side_effects=True, vmem_limit_bytes=VMEM_LIMIT),
    )(which.astype(jnp.int32), slot, queries, key_weight, value_weight, out_weight, database)
    tile = 256
    steps = feats // tile
    return pl.pallas_call(
        project_kernel,
        out_shape=jax.ShapeDtypeStruct((tok, feats), jnp.bfloat16),
        grid_spec=pltpu.PrefetchScalarGridSpec(
            num_scalar_prefetch=1,
            grid=(steps,),
            in_specs=[
                pl.BlockSpec((2, tok, width), lambda i, side: (0, 0, 0)),
                pl.BlockSpec((tile, width), lambda i, side: (side[0] * steps + i, 0)),
                pl.BlockSpec((tile, width), lambda i, side: (i, 0)),
            ],
            out_specs=pl.BlockSpec((tok, tile), lambda i, side: (0, i)),
        ),
        compiler_params=pltpu.CompilerParams(vmem_limit_bytes=VMEM_LIMIT),
    )(h.astype(jnp.int32).reshape(1), att, out_weight, ow_recv)


def local_general(queries, key_weight, value_weight, out_weight, database, neighbours, placement):
    shard_count = lax.axis_size("shard")
    shard_self = lax.axis_index("shard")
    tok_rows = queries.shape[0]
    hd_local = queries.shape[1]
    heads_local = hd_local // HD
    per_dev = tok_rows // CH
    blk_local = database.shape[0]
    slots = placement[neighbours]
    needed = slots.reshape(shard_count, per_dev * KNB)
    owners = needed // blk_local
    matches = owners == shard_self
    hits = jnp.any(matches, axis=1)
    which = jnp.sum(jnp.where(matches, needed % blk_local, 0), axis=1)
    outgoing = jnp.where(hits[:, None, None], database[which], jnp.zeros((), jnp.bfloat16))
    arrived = lax.all_to_all(outgoing, "shard", split_axis=0, concat_axis=0, tiled=True)
    own_need = lax.dynamic_slice_in_dim(needed, shard_self, 1, 0)[0]
    half_rows = arrived[own_need // blk_local]
    encoded = lax.all_gather(half_rows, "head", axis=1, tiled=True)
    key_rows, val_rows = (
        lax.all_gather(key_weight, "shard", axis=0, tiled=True),
        lax.all_gather(value_weight, "shard", axis=0, tiled=True),
    )
    key_block = jnp.einsum(
        "brd,de->bre", encoded, key_rows, preferred_element_type=jnp.float32
    ).astype(jnp.bfloat16)
    val_block = jnp.einsum(
        "brd,de->bre", encoded, val_rows, preferred_element_type=jnp.float32
    ).astype(jnp.bfloat16)
    neighbour_len = encoded.shape[1]
    key_heads = key_block.reshape(per_dev, KNB * neighbour_len, heads_local, HD)
    val_heads = val_block.reshape(per_dev, KNB * neighbour_len, heads_local, HD)
    query_pad = jnp.concatenate(
        [queries[CH - 1 :], jnp.zeros((CH - 1, hd_local), jnp.bfloat16)], axis=0
    )
    query_pad = query_pad.reshape(per_dev, CH, heads_local, HD)
    score_scale = HD ** (-0.5)
    scores = (
        jnp.einsum("swhd,skhd->shwk", query_pad, key_heads, preferred_element_type=jnp.float32)
        * score_scale
    )
    row_max = jnp.max(scores, axis=-1, keepdims=True)
    expo = jnp.exp(scores - row_max)
    probs = expo / jnp.sum(expo, axis=-1, keepdims=True)
    weights_bf = probs.astype(jnp.bfloat16)
    window_out = jnp.einsum(
        "shwk,skhd->swhd", weights_bf, val_heads, preferred_element_type=jnp.float32
    )
    window_rows = window_out.astype(jnp.bfloat16).reshape(tok_rows, hd_local)
    attention = jnp.concatenate(
        [jnp.zeros((CH - 1, hd_local), jnp.bfloat16), window_rows[: tok_rows - (CH - 1)]], axis=0
    )
    partial_value = lax.dot_general(
        attention, out_weight, (((1,), (1,)), ((), ())), preferred_element_type=jnp.float32
    )
    return lax.psum_scatter(partial_value, "head", scatter_dimension=1, tiled=True).astype(
        jnp.bfloat16
    )


def solution(mesh):
    sizes = dict(mesh.shape)
    small = sizes["shard"] == NZ * NY * NX and sizes["head"] == 2
    return jax.shard_map(
        local_small if small else local_general,
        mesh=mesh,
        in_specs=(
            P("shard", "head"),
            P("shard", "head"),
            P("shard", "head"),
            P(None, "head"),
            P("shard", "head", None),
            P(),
            P(),
        ),
        out_specs=P("shard", "head"),
        check_vma=False,
    )
```

```python
import jax
import jax.numpy as jnp
from jax import lax
from jax.experimental import pallas as pl
from jax.experimental.pallas import tpu as pltpu
from jax.sharding import PartitionSpec as P

HD = 128
CH = 64
KNB = 2
NZ, NY, NX = 4, 2, 2
MESH = pl.DeviceIdType.MESH
VMEM_LIMIT = 60 * 1024 * 1024
NT = (((1,), (1,)), ((), ()))


def shifted(shard, dz, dy, dx):
    z, y, x = shard // (NY * NX), (shard // NX) % NY, shard % NX
    return ((z + dz) % NZ) * (NY * NX) + ((y + dy) % NY) * NX + (x + dx) % NX


def fused_kernel(
    which_ref, slot_ref, q_ref, kw_ref, vw_ref, ow_ref, db_ref,
    att_ref, ow_recv,
    w, up_1, up_2, up_3, down_1, down_2, down_3, e_out, e_in, kk, vv,
    d_send, d_recv, a_send, a_recv, f_send, f_recv, z_send, p_send, g_send, w_recv, o_sem,
    t_send, t_recv,
):
    s = lax.axis_index("shard")
    h = lax.axis_index("head")
    z, y, x = s // (NY * NX), (s // NX) % NY, s % NX
    near_x = s + 1 - 2 * x
    near_y = s + NX * (1 - 2 * y)
    plane = NY * NX
    n = NZ * NY * NX
    half, de = db_ref.shape[1], db_ref.shape[2]
    width = q_ref.shape[1]
    feats = ow_recv.shape[0]

    barrier = pltpu.get_barrier_semaphore()
    for d in range(1, n):
        to = shifted(s, d // plane, (d // NX) % NY, d % NX)
        pl.semaphore_signal(barrier, inc=1, device_id=(to, h), device_id_type=MESH)
    pl.semaphore_signal(barrier, inc=1, device_id=(s, 1 - h), device_id_type=MESH)
    w[0, s] = kw_ref[...]
    w[1, s] = vw_ref[...]
    pl.semaphore_wait(barrier, n)
    ups = (db_ref, up_1, up_2, up_3)
    downs = (db_ref, down_1, down_2, down_3)

    def weight_copy(kind, chunk, to, sem):
        return pltpu.make_async_remote_copy(
            src_ref=w.at[kind, chunk], dst_ref=w.at[kind, chunk], send_sem=sem,
            recv_sem=w_recv.at[kind, chunk], device_id=(to, h), device_id_type=MESH)

    def up_copy(kind, zz):
        return weight_copy(kind, zz * plane + y * NX + x, s + plane, z_send.at[0, kind, zz])

    def down_copy(kind, zz):
        return weight_copy(kind, zz * plane + y * NX + x, s - plane, z_send.at[1, kind, zz])

    def x_copy(kind, zz):
        return weight_copy(kind, zz * plane + y * NX + x, near_x, p_send.at[0, kind, zz])

    def y_copy(kind, zz):
        return weight_copy(kind, zz * plane + y * NX + x, near_y, p_send.at[1, kind, zz])

    def diag_k(zz):
        return weight_copy(0, zz * plane + y * NX + 1 - x, near_y, g_send.at[0, zz])

    def diag_v(zz):
        return weight_copy(1, zz * plane + (1 - y) * NX + x, near_x, g_send.at[1, zz])

    def arrive(kind, chunk):
        weight_copy(kind, chunk, near_x, z_send.at[0, 0, 0]).wait_recv()

    def set_up(k):
        return pltpu.make_async_remote_copy(
            src_ref=ups[k], dst_ref=ups[k + 1], send_sem=d_send.at[0, k],
            recv_sem=d_recv.at[0, k + 1], device_id=(s + plane, h), device_id_type=MESH)

    def set_down(k):
        return pltpu.make_async_remote_copy(
            src_ref=downs[k], dst_ref=downs[k + 1], send_sem=d_send.at[1, k],
            recv_sem=d_recv.at[1, k + 1], device_id=(s - plane, h), device_id_type=MESH)

    def enc_copy(zz, j):
        to = shifted(s, 0, j // NX, j % NX)
        d = zz * plane + j
        return pltpu.make_async_remote_copy(
            src_ref=e_out.at[d], dst_ref=e_in.at[d, h], send_sem=a_send.at[d],
            recv_sem=a_recv.at[d], device_id=(to, h), device_id_type=MESH)

    def spread(zz, held):
        for j in range(1, plane):
            d = zz * plane + j
            e_out[d] = held[which_ref[d]]
            enc_copy(zz, j).start()
        e_in[zz * plane, h] = held[which_ref[zz * plane]]
        half_copy(zz * plane).start()

    def hand_on(k):
        @pl.when(z >= k)
        def _():
            set_up(k - 1).wait_recv()
            if k < NZ - 1:
                @pl.when(z < NZ - 1)
                def _():
                    set_up(k).start()

        @pl.when(z + k < NZ)
        def _():
            set_down(k - 1).wait_recv()
            if k < NZ - 1:
                @pl.when(z > 0)
                def _():
                    set_down(k).start()

    def spread_sets(k):
        @pl.when(z >= k)
        def _():
            spread(z - k, ups[k])

        @pl.when(z + k < NZ)
        def _():
            spread(z + k, downs[k])

    def half_copy(d):
        return pltpu.make_async_remote_copy(
            src_ref=e_in.at[d, h], dst_ref=e_in.at[d, h], send_sem=f_send.at[d],
            recv_sem=f_recv.at[d], device_id=(s, 1 - h), device_id_type=MESH)

    def half_arrive(d):
        pltpu.make_async_remote_copy(
            src_ref=e_in.at[d, 1 - h], dst_ref=e_in.at[d, 1 - h], send_sem=f_send.at[d],
            recv_sem=f_recv.at[d], device_id=(s, 1 - h), device_id_type=MESH).wait_recv()

    def out_copy():
        return pltpu.make_async_remote_copy(
            src_ref=ow_ref.at[pl.ds((1 - h) * feats, feats), :], dst_ref=ow_recv,
            send_sem=o_sem.at[0], recv_sem=o_sem.at[1], device_id=(s, 1 - h),
            device_id_type=MESH)

    for kind in range(2):
        @pl.when(z < NZ - 1)
        def _():
            up_copy(kind, z).start()

        @pl.when(z > 0)
        def _():
            down_copy(kind, z).start()
        x_copy(kind, z).start()
        y_copy(kind, z).start()
    out_copy().start()

    def turn(zz):
        arrive(0, zz * plane + y * NX + 1 - x)
        diag_k(zz).start()
        arrive(1, zz * plane + (1 - y) * NX + x)
        diag_v(zz).start()

    def pass_halves(zz):
        for j in range(1, plane):
            enc_copy(zz, j).wait_recv()
            half_copy(zz * plane + j).start()

    for k in range(1, NZ + 1):
        if k < NZ:
            @pl.when(z >= k)
            def _():
                for kind in range(2):
                    arrive(kind, (z - k) * plane + y * NX + x)

                    @pl.when(z < NZ - 1)
                    def _():
                        up_copy(kind, z - k).start()
                    x_copy(kind, z - k).start()
                    y_copy(kind, z - k).start()

            @pl.when(z + k < NZ)
            def _():
                for kind in range(2):
                    arrive(kind, (z + k) * plane + y * NX + x)

                    @pl.when(z > 0)
                    def _():
                        down_copy(kind, z + k).start()
                    x_copy(kind, z + k).start()
                    y_copy(kind, z + k).start()
        if k == 1:
            @pl.when(z < NZ - 1)
            def _():
                set_up(0).start()

            @pl.when(z > 0)
            def _():
                set_down(0).start()
            turn(z)
        else:
            @pl.when(z >= k - 1)
            def _():
                turn(z - (k - 1))

            @pl.when(z + k - 1 < NZ)
            def _():
                turn(z + k - 1)
        if k == 2:
            hand_on(1)
    spread(z, db_ref)
    spread_sets(1)
    hand_on(2)
    spread_sets(2)
    for zz in range(NZ):
        arrive(1, zz * plane + y * NX + 1 - x)
        arrive(0, zz * plane + (1 - y) * NX + x)
        for kind in range(2):
            arrive(kind, zz * plane + (1 - y) * NX + 1 - x)

    tile = 256

    def project(zz):
        for j in range(plane):
            half_arrive(zz * plane + j)
        slab = pl.ds(zz * plane, plane)

        @pl.loop(0, width // tile)
        def _(c):
            cols = pl.ds(pl.multiple_of(c * tile, tile), tile)
            enc = e_in[slab].reshape(plane * 2 * half, de)
            for kind, dst in ((0, kk), (1, vv)):
                rows = w[kind, :, :, cols].reshape(de, tile)
                got = jnp.dot(enc, rows, preferred_element_type=jnp.float32)
                dst[slab, :, cols] = got.astype(jnp.bfloat16).reshape(plane, 2 * half, tile)

    def each(k, act):
        @pl.when(z >= k)
        def _():
            act(z - k)

        @pl.when(z + k < NZ)
        def _():
            act(z + k)

    pass_halves(z)
    project(z)
    for k in range(1, NZ):
        each(k, pass_halves)
        if k == NZ - 2:
            hand_on(NZ - 1)
            spread_sets(NZ - 1)
        each(k, project)

    scale = HD ** -0.5
    groups = q_ref.shape[0] // CH
    edge = 16

    def attend(c, start, count):
        one = slot_ref[KNB * c]
        two = slot_ref[KNB * c + 1]
        last = lax.broadcasted_iota(jnp.int32, (edge, HD), 0) == edge - 1
        batch = 4
        for first in range(0, width // HD, batch):
            spans = [slice(i * HD, (i + 1) * HD) for i in range(first, first + batch)]
            scores = []
            for cols in spans:
                q = q_ref[pl.ds(start, count), cols]
                keys = jnp.concatenate([kk[one, :, cols], kk[two, :, cols]], axis=0)
                scores.append(
                    lax.dot_general(q, keys, NT, preferred_element_type=jnp.float32) * scale)
            tops = [jnp.max(score, axis=1, keepdims=True) for score in scores]
            expos = [jnp.exp(score - top) for score, top in zip(scores, tops)]
            sums = [jnp.sum(expo, axis=1, keepdims=True) for expo in expos]
            weights = [(expo / total).astype(jnp.bfloat16) for expo, total in zip(expos, sums)]
            outs = []
            for cols, weight in zip(spans, weights):
                value = jnp.concatenate([vv[one, :, cols], vv[two, :, cols]], axis=0)
                outs.append(jnp.dot(weight, value, preferred_element_type=jnp.float32))
            for cols, got in zip(spans, outs):
                old = att_ref[0, pl.ds(start, edge), cols].astype(jnp.float32)
                att_ref[0, pl.ds(start, edge), cols] = jnp.where(last, got[:edge], old).astype(
                    jnp.bfloat16)
                if count > edge:
                    att_ref[0, pl.ds(pl.multiple_of(start + edge, edge), count - edge), cols] = (
                        got[edge:].astype(jnp.bfloat16))

    def swap(c):
        rows = pl.ds(pl.multiple_of(c * CH, CH), CH)
        return pltpu.make_async_remote_copy(
            src_ref=att_ref.at[0, rows], dst_ref=att_ref.at[1, rows], send_sem=t_send.at[c],
            recv_sem=t_recv.at[c], device_id=(s, 1 - h), device_id_type=MESH)

    att_ref[0, 0:CH] = jnp.zeros((CH, width), jnp.bfloat16)

    @pl.loop(0, groups - 1)
    def _(c):
        attend(c, pl.multiple_of(c * CH + CH - edge, edge), CH + edge)
        swap(c).start()

    attend(groups - 1, groups * CH - edge, edge)
    swap(groups - 1).start()

    for zz in range(NZ):
        for kind in range(2):
            @pl.when(z < NZ - 1)
            def _():
                @pl.when(z >= zz)
                def _():
                    up_copy(kind, zz).wait_send()

            @pl.when(z > 0)
            def _():
                @pl.when(z <= zz)
                def _():
                    down_copy(kind, zz).wait_send()
            x_copy(kind, zz).wait_send()
            y_copy(kind, zz).wait_send()
        diag_k(zz).wait_send()
        diag_v(zz).wait_send()
    for k in range(NZ - 1):
        @pl.when(z < NZ - 1)
        def _():
            @pl.when(z >= k)
            def _():
                set_up(k).wait_send()

        @pl.when(z > 0)
        def _():
            @pl.when(z + k < NZ)
            def _():
                set_down(k).wait_send()
    for zz in range(NZ):
        for j in range(plane):
            if j:
                enc_copy(zz, j).wait_send()
            half_copy(zz * plane + j).wait_send()
    out_copy().wait()
    for c in range(groups):
        swap(c).wait()


def project_kernel(side_ref, att_ref, own_ref, other_ref, out_ref):
    out_ref[...] = (
        lax.dot_general(att_ref[0], own_ref[...], NT, preferred_element_type=jnp.float32)
        + lax.dot_general(att_ref[1], other_ref[...], NT, preferred_element_type=jnp.float32)
    ).astype(jnp.bfloat16)


def local_small(queries, key_weight, value_weight, out_weight, database, neighbours, placement):
    n = NZ * NY * NX
    s = lax.axis_index("shard")
    h = lax.axis_index("head")
    tok, width = queries.shape
    blk, half, de = database.shape
    feats = out_weight.shape[0] // 2
    nblocks = placement.shape[0]
    ids = jnp.arange(nblocks, dtype=jnp.int32)
    needed = neighbours.reshape(n, -1)
    slots = jnp.sum(jnp.where(needed[:, :, None] == ids, placement, 0), axis=-1)
    owners = slots // blk
    offs = jnp.arange(n, dtype=jnp.int32)
    plane = NY * NX
    dests = shifted(s, 0, (offs // NX) % NY, offs % NX)
    origin = offs // plane * plane + s % plane
    pick = (dests[:, None, None] == offs[None, :, None]) & (owners[None] == origin[:, None, None])
    which = jnp.sum(jnp.where(pick, (slots % blk)[None], 0), axis=(1, 2))
    own = jnp.sum(jnp.where((offs == s)[:, None], owners, 0), axis=0)
    slot = (
        own // plane * plane + (s // NX + own // NX) % NY * NX + (s + own) % NX
    ).astype(jnp.int32)
    vm = pl.BlockSpec(memory_space=pltpu.VMEM)
    sm = pl.BlockSpec(memory_space=pltpu.SMEM)
    hbm = pl.BlockSpec(memory_space=pl.ANY)
    dma = pltpu.SemaphoreType.DMA
    att, ow_recv = pl.pallas_call(
        fused_kernel,
        out_shape=(
            jax.ShapeDtypeStruct((2, tok, width), jnp.bfloat16),
            jax.ShapeDtypeStruct((feats, width), jnp.bfloat16),
        ),
        in_specs=[sm, sm, vm, vm, vm, hbm, vm],
        out_specs=(vm, hbm),
        scratch_shapes=[
            pltpu.VMEM((2, n) + key_weight.shape, jnp.bfloat16),
            *[pltpu.VMEM(database.shape, jnp.bfloat16)] * 6,
            pltpu.VMEM((n, half, de), jnp.bfloat16),
            pltpu.VMEM((n, 2, half, de), jnp.bfloat16),
            pltpu.VMEM((n, 2 * half, width), jnp.bfloat16),
            pltpu.VMEM((n, 2 * half, width), jnp.bfloat16),
            dma((2, NZ)), dma((2, NZ)), dma((n,)), dma((n,)), dma((n,)), dma((n,)),
            dma((2, 2, NZ)), dma((2, 2, NZ)), dma((2, NZ)), dma((2, n)),
            dma((2,)), dma((tok // CH,)), dma((tok // CH,)),
        ],
        compiler_params=pltpu.CompilerParams(
            collective_id=0, has_side_effects=True, vmem_limit_bytes=VMEM_LIMIT),
    )(which.astype(jnp.int32), slot, queries, key_weight, value_weight, out_weight, database)
    tile = 512
    steps = feats // tile
    return pl.pallas_call(
        project_kernel,
        out_shape=jax.ShapeDtypeStruct((tok, feats), jnp.bfloat16),
        grid_spec=pltpu.PrefetchScalarGridSpec(
            num_scalar_prefetch=1,
            grid=(steps,),
            in_specs=[
                pl.BlockSpec((2, tok, width), lambda i, side: (0, 0, 0)),
                pl.BlockSpec((tile, width), lambda i, side: (side[0] * steps + i, 0)),
                pl.BlockSpec((tile, width), lambda i, side: (i, 0)),
            ],
            out_specs=pl.BlockSpec((tok, tile), lambda i, side: (0, i)),
        ),
        compiler_params=pltpu.CompilerParams(vmem_limit_bytes=VMEM_LIMIT),
    )(h.astype(jnp.int32).reshape(1), att, out_weight, ow_recv)


def local_general(queries, key_weight, value_weight, out_weight, database, neighbours, placement):
    shard_count = lax.axis_size("shard")
    shard_self = lax.axis_index("shard")
    tok_rows = queries.shape[0]
    hd_local = queries.shape[1]
    heads_local = hd_local // HD
    per_dev = tok_rows // CH
    blk_local = database.shape[0]
    slots = placement[neighbours]
    needed = slots.reshape(shard_count, per_dev * KNB)
    owners = needed // blk_local
    matches = owners == shard_self
    hits = jnp.any(matches, axis=1)
    which = jnp.sum(jnp.where(matches, needed % blk_local, 0), axis=1)
    outgoing = jnp.where(hits[:, None, None], database[which], jnp.zeros((), jnp.bfloat16))
    arrived = lax.all_to_all(outgoing, "shard", split_axis=0, concat_axis=0, tiled=True)
    own_need = lax.dynamic_slice_in_dim(needed, shard_self, 1, 0)[0]
    half_rows = arrived[own_need // blk_local]
    encoded = lax.all_gather(half_rows, "head", axis=1, tiled=True)
    key_rows, val_rows = (
        lax.all_gather(key_weight, "shard", axis=0, tiled=True),
        lax.all_gather(value_weight, "shard", axis=0, tiled=True),
    )
    key_block = jnp.einsum(
        "brd,de->bre", encoded, key_rows, preferred_element_type=jnp.float32
    ).astype(jnp.bfloat16)
    val_block = jnp.einsum(
        "brd,de->bre", encoded, val_rows, preferred_element_type=jnp.float32
    ).astype(jnp.bfloat16)
    neighbour_len = encoded.shape[1]
    key_heads = key_block.reshape(per_dev, KNB * neighbour_len, heads_local, HD)
    val_heads = val_block.reshape(per_dev, KNB * neighbour_len, heads_local, HD)
    query_pad = jnp.concatenate(
        [queries[CH - 1 :], jnp.zeros((CH - 1, hd_local), jnp.bfloat16)], axis=0
    )
    query_pad = query_pad.reshape(per_dev, CH, heads_local, HD)
    score_scale = HD ** (-0.5)
    scores = (
        jnp.einsum("swhd,skhd->shwk", query_pad, key_heads, preferred_element_type=jnp.float32)
        * score_scale
    )
    row_max = jnp.max(scores, axis=-1, keepdims=True)
    expo = jnp.exp(scores - row_max)
    probs = expo / jnp.sum(expo, axis=-1, keepdims=True)
    weights_bf = probs.astype(jnp.bfloat16)
    window_out = jnp.einsum(
        "shwk,skhd->swhd", weights_bf, val_heads, preferred_element_type=jnp.float32
    )
    window_rows = window_out.astype(jnp.bfloat16).reshape(tok_rows, hd_local)
    attention = jnp.concatenate(
        [jnp.zeros((CH - 1, hd_local), jnp.bfloat16), window_rows[: tok_rows - (CH - 1)]], axis=0
    )
    partial_value = lax.dot_general(
        attention, out_weight, (((1,), (1,)), ((), ())), preferred_element_type=jnp.float32
    )
    return lax.psum_scatter(partial_value, "head", scatter_dimension=1, tiled=True).astype(
        jnp.bfloat16
    )


def solution(mesh):
    sizes = dict(mesh.shape)
    small = sizes["shard"] == NZ * NY * NX and sizes["head"] == 2
    return jax.shard_map(
        local_small if small else local_general,
        mesh=mesh,
        in_specs=(
            P("shard", "head"),
            P("shard", "head"),
            P("shard", "head"),
            P(None, "head"),
            P("shard", "head", None),
            P(),
            P(),
        ),
        out_specs=P("shard", "head"),
        check_vma=False,
    )
```

```python
import jax
import jax.numpy as jnp
from jax import lax
from jax.experimental import pallas as pl
from jax.experimental.pallas import tpu as pltpu
from jax.sharding import PartitionSpec as P

HD = 128
CH = 64
KNB = 2
NZ, NY, NX = 4, 2, 2
MESH = pl.DeviceIdType.MESH
VMEM_LIMIT = 60 * 1024 * 1024
NT = (((1,), (1,)), ((), ()))


def shifted(shard, dz, dy, dx):
    z, y, x = shard // (NY * NX), (shard // NX) % NY, shard % NX
    return ((z + dz) % NZ) * (NY * NX) + ((y + dy) % NY) * NX + (x + dx) % NX


def fused_kernel(
    near_ref, place_ref, q_ref, kw_ref, vw_ref, ow_ref, db_ref,
    att_ref, ow_recv,
    w, up_1, up_2, up_3, down_1, down_2, down_3, e_out, e_in, kk, vv,
    d_send, d_recv, a_send, a_recv, f_send, f_recv, z_send, p_send, g_send, w_recv, o_sem,
    t_send, t_recv,
):
    s = lax.axis_index("shard")
    h = lax.axis_index("head")
    z, y, x = s // (NY * NX), (s // NX) % NY, s % NX
    near_x = s + 1 - 2 * x
    near_y = s + NX * (1 - 2 * y)
    plane = NY * NX
    n = NZ * NY * NX
    half, de = db_ref.shape[1], db_ref.shape[2]
    width = q_ref.shape[1]
    feats = ow_recv.shape[0]

    barrier = pltpu.get_barrier_semaphore()
    for d in range(1, n):
        to = shifted(s, d // plane, (d // NX) % NY, d % NX)
        pl.semaphore_signal(barrier, inc=1, device_id=(to, h), device_id_type=MESH)
    pl.semaphore_signal(barrier, inc=1, device_id=(s, 1 - h), device_id_type=MESH)
    w[0, s] = kw_ref[...]
    w[1, s] = vw_ref[...]
    pl.semaphore_wait(barrier, n)
    ups = (db_ref, up_1, up_2, up_3)
    downs = (db_ref, down_1, down_2, down_3)

    def weight_copy(kind, chunk, to, sem):
        return pltpu.make_async_remote_copy(
            src_ref=w.at[kind, chunk], dst_ref=w.at[kind, chunk], send_sem=sem,
            recv_sem=w_recv.at[kind, chunk], device_id=(to, h), device_id_type=MESH)

    def up_copy(kind, zz):
        return weight_copy(kind, zz * plane + y * NX + x, s + plane, z_send.at[0, kind, zz])

    def down_copy(kind, zz):
        return weight_copy(kind, zz * plane + y * NX + x, s - plane, z_send.at[1, kind, zz])

    def x_copy(kind, zz):
        return weight_copy(kind, zz * plane + y * NX + x, near_x, p_send.at[0, kind, zz])

    def y_copy(kind, zz):
        return weight_copy(kind, zz * plane + y * NX + x, near_y, p_send.at[1, kind, zz])

    def diag_k(zz):
        return weight_copy(0, zz * plane + y * NX + 1 - x, near_y, g_send.at[0, zz])

    def diag_v(zz):
        return weight_copy(1, zz * plane + (1 - y) * NX + x, near_x, g_send.at[1, zz])

    def arrive(kind, chunk):
        weight_copy(kind, chunk, near_x, z_send.at[0, 0, 0]).wait_recv()

    def set_up(k):
        return pltpu.make_async_remote_copy(
            src_ref=ups[k], dst_ref=ups[k + 1], send_sem=d_send.at[0, k],
            recv_sem=d_recv.at[0, k + 1], device_id=(s + plane, h), device_id_type=MESH)

    def set_down(k):
        return pltpu.make_async_remote_copy(
            src_ref=downs[k], dst_ref=downs[k + 1], send_sem=d_send.at[1, k],
            recv_sem=d_recv.at[1, k + 1], device_id=(s - plane, h), device_id_type=MESH)

    def enc_copy(zz, j):
        to = shifted(s, 0, j // NX, j % NX)
        d = zz * plane + j
        return pltpu.make_async_remote_copy(
            src_ref=e_out.at[d], dst_ref=e_in.at[d, h], send_sem=a_send.at[d],
            recv_sem=a_recv.at[d], device_id=(to, h), device_id_type=MESH)

    def spread(zz, held):
        for j in range(1, plane):
            d = zz * plane + j
            e_out[d] = held[chosen(zz, j)]
            enc_copy(zz, j).start()
        e_in[zz * plane, h] = held[chosen(zz, 0)]
        half_copy(zz * plane).start()

    def hand_on(k):
        @pl.when(z >= k)
        def _():
            set_up(k - 1).wait_recv()
            if k < NZ - 1:
                @pl.when(z < NZ - 1)
                def _():
                    set_up(k).start()

        @pl.when(z + k < NZ)
        def _():
            set_down(k - 1).wait_recv()
            if k < NZ - 1:
                @pl.when(z > 0)
                def _():
                    set_down(k).start()

    def spread_sets(k):
        @pl.when(z >= k)
        def _():
            spread(z - k, ups[k])

        @pl.when(z + k < NZ)
        def _():
            spread(z + k, downs[k])

    picks = near_ref.shape[0] // n
    blk = db_ref.shape[0]

    def find(j):
        to = shifted(s, 0, j // NX, j % NX)
        found = [jnp.int32(0)] * NZ
        for i in range(picks):
            stored = place_ref[near_ref[to * picks + i]]
            owner, block = stored // blk, stored % blk
            found = [
                got + jnp.where(owner == zz * plane + s % plane, block, 0)
                for zz, got in enumerate(found)]
        return found

    def slot_of(i):
        own = place_ref[near_ref[s * picks + i]] // blk
        return own // plane * plane + (y + own // NX) % NY * NX + (x + own) % NX

    def half_copy(d):
        return pltpu.make_async_remote_copy(
            src_ref=e_in.at[d, h], dst_ref=e_in.at[d, h], send_sem=f_send.at[d],
            recv_sem=f_recv.at[d], device_id=(s, 1 - h), device_id_type=MESH)

    def half_arrive(d):
        pltpu.make_async_remote_copy(
            src_ref=e_in.at[d, 1 - h], dst_ref=e_in.at[d, 1 - h], send_sem=f_send.at[d],
            recv_sem=f_recv.at[d], device_id=(s, 1 - h), device_id_type=MESH).wait_recv()

    def out_copy():
        return pltpu.make_async_remote_copy(
            src_ref=ow_ref.at[pl.ds((1 - h) * feats, feats), :], dst_ref=ow_recv,
            send_sem=o_sem.at[0], recv_sem=o_sem.at[1], device_id=(s, 1 - h),
            device_id_type=MESH)

    for kind in range(2):
        @pl.when(z < NZ - 1)
        def _():
            up_copy(kind, z).start()

        @pl.when(z > 0)
        def _():
            down_copy(kind, z).start()
        x_copy(kind, z).start()
        y_copy(kind, z).start()
    out_copy().start()
    blocks = [find(j) for j in range(plane)]

    def chosen(zz, j):
        return sum(jnp.where(zz == i, got, 0) for i, got in enumerate(blocks[j]))


    def turn(zz):
        arrive(0, zz * plane + y * NX + 1 - x)
        diag_k(zz).start()
        arrive(1, zz * plane + (1 - y) * NX + x)
        diag_v(zz).start()

    def pass_halves(zz):
        for j in range(1, plane):
            enc_copy(zz, j).wait_recv()
            half_copy(zz * plane + j).start()

    for k in range(1, NZ + 1):
        if k < NZ:
            @pl.when(z >= k)
            def _():
                for kind in range(2):
                    arrive(kind, (z - k) * plane + y * NX + x)

                    @pl.when(z < NZ - 1)
                    def _():
                        up_copy(kind, z - k).start()
                    x_copy(kind, z - k).start()
                    y_copy(kind, z - k).start()

            @pl.when(z + k < NZ)
            def _():
                for kind in range(2):
                    arrive(kind, (z + k) * plane + y * NX + x)

                    @pl.when(z > 0)
                    def _():
                        down_copy(kind, z + k).start()
                    x_copy(kind, z + k).start()
                    y_copy(kind, z + k).start()
        if k == 1:
            @pl.when(z < NZ - 1)
            def _():
                set_up(0).start()

            @pl.when(z > 0)
            def _():
                set_down(0).start()
            turn(z)
        else:
            @pl.when(z >= k - 1)
            def _():
                turn(z - (k - 1))

            @pl.when(z + k - 1 < NZ)
            def _():
                turn(z + k - 1)
        if k == 2:
            hand_on(1)
    spread(z, db_ref)
    spread_sets(1)
    hand_on(2)
    spread_sets(2)
    for zz in range(NZ):
        arrive(1, zz * plane + y * NX + 1 - x)
        arrive(0, zz * plane + (1 - y) * NX + x)
        for kind in range(2):
            arrive(kind, zz * plane + (1 - y) * NX + 1 - x)

    tile = 256

    def project(zz):
        for j in range(plane):
            half_arrive(zz * plane + j)
        slab = pl.ds(zz * plane, plane)

        @pl.loop(0, width // tile)
        def _(c):
            cols = pl.ds(pl.multiple_of(c * tile, tile), tile)
            enc = e_in[slab].reshape(plane * 2 * half, de)
            for kind, dst in ((0, kk), (1, vv)):
                rows = w[kind, :, :, cols].reshape(de, tile)
                got = jnp.dot(enc, rows, preferred_element_type=jnp.float32)
                dst[slab, :, cols] = got.astype(jnp.bfloat16).reshape(plane, 2 * half, tile)

    def each(k, act):
        @pl.when(z >= k)
        def _():
            act(z - k)

        @pl.when(z + k < NZ)
        def _():
            act(z + k)

    pass_halves(z)
    project(z)
    for k in range(1, NZ):
        each(k, pass_halves)
        if k == NZ - 2:
            hand_on(NZ - 1)
            spread_sets(NZ - 1)
        each(k, project)

    scale = HD ** -0.5
    groups = q_ref.shape[0] // CH
    edge = 16

    def attend(c, start, count):
        one = slot_of(KNB * c)
        two = slot_of(KNB * c + 1)
        last = lax.broadcasted_iota(jnp.int32, (edge, HD), 0) == edge - 1
        batch = 4
        for first in range(0, width // HD, batch):
            spans = [slice(i * HD, (i + 1) * HD) for i in range(first, first + batch)]
            scores = []
            for cols in spans:
                q = q_ref[pl.ds(start, count), cols]
                keys = jnp.concatenate([kk[one, :, cols], kk[two, :, cols]], axis=0)
                scores.append(
                    lax.dot_general(q, keys, NT, preferred_element_type=jnp.float32) * scale)
            tops = [jnp.max(score, axis=1, keepdims=True) for score in scores]
            expos = [jnp.exp(score - top) for score, top in zip(scores, tops)]
            sums = [jnp.sum(expo, axis=1, keepdims=True) for expo in expos]
            weights = [(expo / total).astype(jnp.bfloat16) for expo, total in zip(expos, sums)]
            outs = []
            for cols, weight in zip(spans, weights):
                value = jnp.concatenate([vv[one, :, cols], vv[two, :, cols]], axis=0)
                outs.append(jnp.dot(weight, value, preferred_element_type=jnp.float32))
            for cols, got in zip(spans, outs):
                old = att_ref[0, pl.ds(start, edge), cols].astype(jnp.float32)
                att_ref[0, pl.ds(start, edge), cols] = jnp.where(last, got[:edge], old).astype(
                    jnp.bfloat16)
                if count > edge:
                    att_ref[0, pl.ds(pl.multiple_of(start + edge, edge), count - edge), cols] = (
                        got[edge:].astype(jnp.bfloat16))

    def swap(c):
        rows = pl.ds(pl.multiple_of(c * CH, CH), CH)
        return pltpu.make_async_remote_copy(
            src_ref=att_ref.at[0, rows], dst_ref=att_ref.at[1, rows], send_sem=t_send.at[c],
            recv_sem=t_recv.at[c], device_id=(s, 1 - h), device_id_type=MESH)

    att_ref[0, 0:CH] = jnp.zeros((CH, width), jnp.bfloat16)

    @pl.loop(0, groups - 1)
    def _(c):
        attend(c, pl.multiple_of(c * CH + CH - edge, edge), CH + edge)
        swap(c).start()

    attend(groups - 1, groups * CH - edge, edge)
    swap(groups - 1).start()

    for zz in range(NZ):
        for kind in range(2):
            @pl.when(z < NZ - 1)
            def _():
                @pl.when(z >= zz)
                def _():
                    up_copy(kind, zz).wait_send()

            @pl.when(z > 0)
            def _():
                @pl.when(z <= zz)
                def _():
                    down_copy(kind, zz).wait_send()
            x_copy(kind, zz).wait_send()
            y_copy(kind, zz).wait_send()
        diag_k(zz).wait_send()
        diag_v(zz).wait_send()
    for k in range(NZ - 1):
        @pl.when(z < NZ - 1)
        def _():
            @pl.when(z >= k)
            def _():
                set_up(k).wait_send()

        @pl.when(z > 0)
        def _():
            @pl.when(z + k < NZ)
            def _():
                set_down(k).wait_send()
    for zz in range(NZ):
        for j in range(plane):
            if j:
                enc_copy(zz, j).wait_send()
            half_copy(zz * plane + j).wait_send()
    out_copy().wait()
    for c in range(groups):
        swap(c).wait()


def project_kernel(side_ref, att_ref, own_ref, other_ref, out_ref):
    out_ref[...] = (
        lax.dot_general(att_ref[0], own_ref[...], NT, preferred_element_type=jnp.float32)
        + lax.dot_general(att_ref[1], other_ref[...], NT, preferred_element_type=jnp.float32)
    ).astype(jnp.bfloat16)


def local_small(queries, key_weight, value_weight, out_weight, database, neighbours, placement):
    n = NZ * NY * NX
    h = lax.axis_index("head")
    tok, width = queries.shape
    half, de = database.shape[1:]
    feats = out_weight.shape[0] // 2
    vm = pl.BlockSpec(memory_space=pltpu.VMEM)
    sm = pl.BlockSpec(memory_space=pltpu.SMEM)
    hbm = pl.BlockSpec(memory_space=pl.ANY)
    dma = pltpu.SemaphoreType.DMA
    att, ow_recv = pl.pallas_call(
        fused_kernel,
        out_shape=(
            jax.ShapeDtypeStruct((2, tok, width), jnp.bfloat16),
            jax.ShapeDtypeStruct((feats, width), jnp.bfloat16),
        ),
        in_specs=[sm, sm, vm, vm, vm, hbm, vm],
        out_specs=(vm, hbm),
        scratch_shapes=[
            pltpu.VMEM((2, n) + key_weight.shape, jnp.bfloat16),
            *[pltpu.VMEM(database.shape, jnp.bfloat16)] * 6,
            pltpu.VMEM((n, half, de), jnp.bfloat16),
            pltpu.VMEM((n, 2, half, de), jnp.bfloat16),
            pltpu.VMEM((n, 2 * half, width), jnp.bfloat16),
            pltpu.VMEM((n, 2 * half, width), jnp.bfloat16),
            dma((2, NZ)), dma((2, NZ)), dma((n,)), dma((n,)), dma((n,)), dma((n,)),
            dma((2, 2, NZ)), dma((2, 2, NZ)), dma((2, NZ)), dma((2, n)),
            dma((2,)), dma((tok // CH,)), dma((tok // CH,)),
        ],
        compiler_params=pltpu.CompilerParams(
            collective_id=0, has_side_effects=True, vmem_limit_bytes=VMEM_LIMIT),
    )(neighbours.reshape(-1), placement, queries, key_weight, value_weight, out_weight, database)
    tile = 512
    steps = feats // tile
    return pl.pallas_call(
        project_kernel,
        out_shape=jax.ShapeDtypeStruct((tok, feats), jnp.bfloat16),
        grid_spec=pltpu.PrefetchScalarGridSpec(
            num_scalar_prefetch=1,
            grid=(steps,),
            in_specs=[
                pl.BlockSpec((2, tok, width), lambda i, side: (0, 0, 0)),
                pl.BlockSpec((tile, width), lambda i, side: (side[0] * steps + i, 0)),
                pl.BlockSpec((tile, width), lambda i, side: (i, 0)),
            ],
            out_specs=pl.BlockSpec((tok, tile), lambda i, side: (0, i)),
        ),
        compiler_params=pltpu.CompilerParams(vmem_limit_bytes=VMEM_LIMIT),
    )(h.astype(jnp.int32).reshape(1), att, out_weight, ow_recv)


def local_general(queries, key_weight, value_weight, out_weight, database, neighbours, placement):
    shard_count = lax.axis_size("shard")
    shard_self = lax.axis_index("shard")
    tok_rows = queries.shape[0]
    hd_local = queries.shape[1]
    heads_local = hd_local // HD
    per_dev = tok_rows // CH
    blk_local = database.shape[0]
    slots = placement[neighbours]
    needed = slots.reshape(shard_count, per_dev * KNB)
    owners = needed // blk_local
    matches = owners == shard_self
    hits = jnp.any(matches, axis=1)
    which = jnp.sum(jnp.where(matches, needed % blk_local, 0), axis=1)
    outgoing = jnp.where(hits[:, None, None], database[which], jnp.zeros((), jnp.bfloat16))
    arrived = lax.all_to_all(outgoing, "shard", split_axis=0, concat_axis=0, tiled=True)
    own_need = lax.dynamic_slice_in_dim(needed, shard_self, 1, 0)[0]
    half_rows = arrived[own_need // blk_local]
    encoded = lax.all_gather(half_rows, "head", axis=1, tiled=True)
    key_rows, val_rows = (
        lax.all_gather(key_weight, "shard", axis=0, tiled=True),
        lax.all_gather(value_weight, "shard", axis=0, tiled=True),
    )
    key_block = jnp.einsum(
        "brd,de->bre", encoded, key_rows, preferred_element_type=jnp.float32
    ).astype(jnp.bfloat16)
    val_block = jnp.einsum(
        "brd,de->bre", encoded, val_rows, preferred_element_type=jnp.float32
    ).astype(jnp.bfloat16)
    neighbour_len = encoded.shape[1]
    key_heads = key_block.reshape(per_dev, KNB * neighbour_len, heads_local, HD)
    val_heads = val_block.reshape(per_dev, KNB * neighbour_len, heads_local, HD)
    query_pad = jnp.concatenate(
        [queries[CH - 1 :], jnp.zeros((CH - 1, hd_local), jnp.bfloat16)], axis=0
    )
    query_pad = query_pad.reshape(per_dev, CH, heads_local, HD)
    score_scale = HD ** (-0.5)
    scores = (
        jnp.einsum("swhd,skhd->shwk", query_pad, key_heads, preferred_element_type=jnp.float32)
        * score_scale
    )
    row_max = jnp.max(scores, axis=-1, keepdims=True)
    expo = jnp.exp(scores - row_max)
    probs = expo / jnp.sum(expo, axis=-1, keepdims=True)
    weights_bf = probs.astype(jnp.bfloat16)
    window_out = jnp.einsum(
        "shwk,skhd->swhd", weights_bf, val_heads, preferred_element_type=jnp.float32
    )
    window_rows = window_out.astype(jnp.bfloat16).reshape(tok_rows, hd_local)
    attention = jnp.concatenate(
        [jnp.zeros((CH - 1, hd_local), jnp.bfloat16), window_rows[: tok_rows - (CH - 1)]], axis=0
    )
    partial_value = lax.dot_general(
        attention, out_weight, (((1,), (1,)), ((), ())), preferred_element_type=jnp.float32
    )
    return lax.psum_scatter(partial_value, "head", scatter_dimension=1, tiled=True).astype(
        jnp.bfloat16
    )


def solution(mesh):
    sizes = dict(mesh.shape)
    small = sizes["shard"] == NZ * NY * NX and sizes["head"] == 2
    return jax.shard_map(
        local_small if small else local_general,
        mesh=mesh,
        in_specs=(
            P("shard", "head"),
            P("shard", "head"),
            P("shard", "head"),
            P(None, "head"),
            P("shard", "head", None),
            P(),
            P(),
        ),
        out_specs=P("shard", "head"),
        check_vma=False,
    )
```
